32 devices in a mesh: rows: 8 (over z, y), vecs: 4 (over x, core).
Axes of the slice: x: 2, y: 2, z: 4, core: 2. Of those that a mesh axis runs over, the one named last changes fastest.
Arguments:
- vectors: bfloat16 [24576, 512], P('rows', 'vecs'), may hold values from -8 to 8
- node_mass: float32 [24576], P('rows'), may hold values from 0.5 to 2
- cable_stiff: float32 [24576], P('rows'), may hold values from 0.1 to 1
- cable_nodes: int32 [8, 4], P('rows'), may hold values from 1 to 1152, 2304 in all within a row
- deck_rigidity: float32 [], replicated, may hold values from 0.3 to 1
- anchor_rows: int32 [8, 8, 4], P('rows'), may hold values from 0 to 3072, as said below
- anchor_stiff: float32 [8, 8, 4], P('rows'), may hold values from 0.2 to 1, as said below
- cut_low: float32 [], replicated, may hold values from 1.5 to 2.5
- top_bound: float32 [], replicated, may hold values from 7 to 9
Outputs:
- basis: bfloat16 [24576, 512], P('rows', 'vecs')
The draws below stay inside these ranges and needn't reach their ends.
Inputs may be any that keep to these rules, and one draw needn't show every extreme that they name: anchor_rows[r, q, s] is a node of partition r coupled through slot s to partition q, or 3072 where the slot is empty; slot s of r towards q is live exactly when slot s of q towards r is; live slots come first; no partition has live slots towards itself; a partition that is not a pylon partition has live slots only towards the partitions beside it in the cyclic order, which fill all 4 slots, and towards at most 4 pylon partitions; pylon partitions come in pairs half the cyclic order apart, and the two of a pair fill all 4 slots towards each other. anchor_stiff[r, q, s] equals anchor_stiff[q, r, s].
All inputs are finite; a program needn't handle non-finite values.
Results may differ from the reference program's by a relative error of at most 0.0072.
The reference program's roundings to bfloat16 on the way (of `filtered` and `factor`) count: a program that leaves them out, or rounds other values in their place, can miss the bound.
Values may be sent and summed in bfloat16 or wider, within the bound.
A program may use at most 64 MiB of HBM per device.

```python
import math
import jax
import jax.numpy as jnp
import numpy as np

ROWS_DEV = 3072
BLOCK = 512
SLOTS = 4
PYLONS = 4
CAB_DEV = 4
DECK_DEV = 768
CABLE_ROWS = 2304
CABLE_MOST = 1152
PIECES = 8
TOTAL = 24576


def draw_vectors(key, part):
    normal_draw = jax.random.normal(jax.random.fold_in(key, 21), (TOTAL, BLOCK), jnp.float32)
    mixed_draw = normal_draw + 0.6 * jnp.roll(normal_draw, 1, axis=1) + 0.4 * jnp.roll(normal_draw, 2, axis=1)
    heavy_parts = jax.random.permutation(jax.random.fold_in(key, 25), PIECES)[:4]
    owner_part = jnp.arange(TOTAL, dtype=jnp.int32) // ROWS_DEV
    is_heavy = jnp.any(owner_part[:, None] == heavy_parts[None, :], axis=1)
    part_scale = jnp.where(is_heavy, 2.8, 0.7)[:, None]
    mixed_draw = mixed_draw * part_scale
    return jnp.clip(mixed_draw, -8.0, 8.0).astype(jnp.bfloat16)


def anchor_counts(key):
    base_counts = jax.random.randint(jax.random.fold_in(key, 11), (PIECES, PIECES), 1, SLOTS + 1)
    first_index = jnp.arange(PIECES)[:, None]
    second_index = jnp.arange(PIECES)[None, :]
    half_count = PIECES // 2
    pair_base = jax.random.permutation(jax.random.fold_in(key, 14), half_count)[:PYLONS // 2]
    pylon_list = jnp.concatenate([pair_base, pair_base + half_count])
    pick = jax.random.randint(jax.random.fold_in(key, 15), (PIECES,), 0, PYLONS)
    partner = pylon_list[pick]
    linked = partner[:, None] == second_index
    linked = linked | linked.T
    symmetric = jnp.where(first_index < second_index, base_counts, base_counts.T)
    symmetric = jnp.where(linked, symmetric, 0)
    is_pylon = jnp.any(jnp.arange(PIECES)[:, None] == pylon_list[None, :], axis=1)
    opposite = (second_index == (first_index + half_count) % PIECES) & is_pylon[:, None]
    symmetric = jnp.where(opposite, SLOTS, symmetric)
    neighbour = (second_index == (first_index + 1) % PIECES) | (first_index == (second_index + 1) % PIECES)
    symmetric = jnp.where(neighbour, SLOTS, symmetric)
    return jnp.where(first_index == second_index, 0, symmetric)


def draw_anchor_rows(key, part):
    counts = anchor_counts(key)
    picked_rows = jax.random.randint(jax.random.fold_in(key, 12), (PIECES, PIECES, SLOTS), 0, ROWS_DEV)
    live_slots = jnp.arange(SLOTS)[None, None, :] < counts[:, :, None]
    return jnp.where(live_slots, picked_rows, ROWS_DEV).astype(jnp.int32)


def draw_anchor_stiff(key, part):
    spring_draw = jnp.exp(jax.random.uniform(jax.random.fold_in(key, 13), (PIECES, PIECES, SLOTS), jnp.float32, math.log(0.2), 0.0))
    first_index = jnp.arange(PIECES)[:, None, None]
    second_index = jnp.arange(PIECES)[None, :, None]
    symmetric = jnp.where(first_index < second_index, spring_draw, jnp.transpose(spring_draw, (1, 0, 2)))
    return symmetric.astype(jnp.float32)


def levels(key, dims, pieces, smallest, top_value):
    gain = 1.0
    for dim, parts in pieces:
        steps = jax.random.uniform(jax.random.fold_in(jax.random.fold_in(key, 6), dim), (parts,), jnp.float32, smallest / len(pieces), top_value / len(pieces))
        gain = gain * jnp.repeat(jnp.exp(steps), dims[dim] // parts).reshape((-1,) + (1,) * (len(dims) - 1 - dim))
    return gain


def length_profile(amount, total, bound, slope):
    portions = [(1 << 20) // math.isqrt(rank ** slope) + 1 for rank in range(2, amount + 1)]
    rest, given = total - bound - (amount - 1), [1] * (amount - 1)
    while rest > 0:
        candidates = [i for i in range(amount - 1) if given[i] < bound]
        pool, budget = sum([portions[i] for i in candidates]), rest
        for i in candidates:
            addition = min(bound - given[i], max(1, budget * portions[i] // pool), rest)
            given[i] = given[i] + addition
            rest = rest - addition
    return np.array([bound] + given)


def ragged(key, count, total, limit, slope):
    if count == 2:
        one = jax.random.randint(key, (), max(1, total - limit), min(limit, total - 1) + 1)
        return jnp.stack([one, total - one])
    tallies = jnp.asarray(length_profile(count, total, limit, slope), jnp.int32)
    couples = (count - 1) // 2
    donor, sink = tallies[1:1 + 2 * couples:2], tallies[2:2 + 2 * couples:2]
    room = jnp.minimum(donor - 1, limit - sink)
    passed = jax.random.randint(jax.random.fold_in(key, 1), (couples,), 0, 1 << 20) % (room + 1)
    tallies = tallies.at[1:1 + 2 * couples:2].set(donor - passed).at[2:2 + 2 * couples:2].set(sink + passed)
    return tallies[jax.random.permutation(jax.random.fold_in(key, 2), count)]


def setup_inputs(seed: int = 0) -> dict:
    seeds = jax.random.split(jax.random.key(seed), 10)
    vectors = draw_vectors(jax.random.fold_in(seeds[9], 71), 0)
    node_mass = jnp.clip(jnp.exp(math.log(2.0) - 1.3862944 * jax.random.uniform(seeds[1], (TOTAL,), jnp.float32) ** levels(seeds[1], (TOTAL,), ((0, 8),), -0.2, 0.2)), 0.5, 2.0)
    cable_stiff = jnp.clip(jnp.exp(math.log(1.0) - 2.3025851 * jax.random.uniform(seeds[2], (TOTAL,), jnp.float32) ** levels(seeds[2], (TOTAL,), ((0, 8),), -0.2, 0.2)), 0.1, 1.0)
    cable_nodes = jax.vmap(lambda own: ragged(own, CAB_DEV, CABLE_ROWS, CABLE_MOST, 2))(jax.random.split(seeds[3], PIECES)).reshape((PIECES, CAB_DEV)).astype(jnp.int32)
    deck_rigidity = jnp.clip(jax.random.uniform(seeds[4], (), jnp.float32, 0.3, 1.0), 0.3, 1.0)
    anchor_rows = draw_anchor_rows(jax.random.fold_in(seeds[9], 71), 0)
    anchor_stiff = draw_anchor_stiff(jax.random.fold_in(seeds[9], 71), 0)
    cut_low = jnp.clip(jax.random.uniform(seeds[7], (), jnp.float32, 1.5, 2.5), 1.5, 2.5)
    top_bound = jnp.clip(jax.random.uniform(seeds[8], (), jnp.float32, 7.0, 9.0), 7.0, 9.0)
    return {"vectors": vectors, "node_mass": node_mass, "cable_stiff": cable_stiff, "cable_nodes": cable_nodes, "deck_rigidity": deck_rigidity, "anchor_rows": anchor_rows, "anchor_stiff": anchor_stiff, "cut_low": cut_low, "top_bound": top_bound}


def cable_term(values, stiff_rows, cable_nodes):
    cable_ends = jnp.cumsum(cable_nodes, axis=1)
    positions = jnp.arange(CABLE_ROWS - 1, dtype=jnp.int32) + 1
    breaks = jnp.any(positions[None, :, None] == cable_ends[:, None, :], axis=2)
    cable_links = jnp.where(breaks, jnp.zeros_like(stiff_rows[:, :CABLE_ROWS - 1]), stiff_rows[:, :CABLE_ROWS - 1])
    cable_flux = cable_links[:, :, None] * (values[:, :-1] - values[:, 1:])
    return jnp.pad(cable_flux, ((0, 0), (0, 1), (0, 0))) - jnp.pad(cable_flux, ((0, 0), (1, 0), (0, 0)))

def deck_term(values, deck_rigidity):
    chain = values.reshape(PIECES * DECK_DEV, values.shape[2])
    deck_flux = deck_rigidity * (chain[:-1] - chain[1:])
    result = jnp.pad(deck_flux, ((0, 1), (0, 0))) - jnp.pad(deck_flux, ((1, 0), (0, 0)))
    return result.reshape(PIECES, DECK_DEV, values.shape[2])

def anchor_term(values, anchor_rows, anchor_stiff):
    part_index = jnp.arange(PIECES, dtype=jnp.int32)
    remote_rows = jnp.transpose(anchor_rows, (1, 0, 2))
    remote_values = values.at[part_index[None, :, None], remote_rows].get(mode='fill', fill_value=0.0)
    local_values = values.at[part_index[:, None, None], anchor_rows].get(mode='fill', fill_value=0.0)
    anchor_force = anchor_stiff[:, :, :, None] * (local_values - remote_values)
    owners = jnp.broadcast_to(part_index[:, None, None], anchor_rows.shape)
    return jnp.zeros_like(values).at[owners, anchor_rows].add(anchor_force, mode='drop')

def operate(values, mass_rows, stiff_rows, cable_nodes, deck_rigidity, anchor_rows, anchor_stiff):
    cable_side = cable_term(values[:, :CABLE_ROWS], stiff_rows, cable_nodes)
    deck_side = deck_term(values[:, CABLE_ROWS:], deck_rigidity)
    springs = jnp.concatenate([cable_side, deck_side], axis=1)
    return mass_rows[:, :, None] * values + springs + anchor_term(values, anchor_rows, anchor_stiff)

def reference(vectors, node_mass, cable_stiff, cable_nodes, deck_rigidity, anchor_rows, anchor_stiff, cut_low, top_bound):
    mass_rows = node_mass.reshape(PIECES, ROWS_DEV)
    stiff_rows = cable_stiff.reshape(PIECES, ROWS_DEV)
    start_block = vectors.astype(jnp.float32).reshape(PIECES, ROWS_DEV, BLOCK)
    center = (top_bound + cut_low) * 0.5
    half_width = (top_bound - cut_low) * 0.5

    def apply_operator(values):
        return operate(values, mass_rows, stiff_rows, cable_nodes, deck_rigidity, anchor_rows, anchor_stiff)
    first_degree = (apply_operator(start_block) - center * start_block) / half_width
    second_degree = 2.0 * (apply_operator(first_degree) - center * first_degree) / half_width - start_block
    filtered = second_degree.reshape(TOTAL, BLOCK).astype(jnp.bfloat16)
    gram_matrix = jnp.dot(filtered.T.astype(jnp.float32), filtered.astype(jnp.float32), preferred_element_type=jnp.float32) / TOTAL
    lower_factor = jnp.linalg.cholesky(gram_matrix)
    identity = jnp.eye(BLOCK, dtype=jnp.float32)
    inverse = jax.scipy.linalg.solve_triangular(lower_factor, identity, lower=True)
    factor = inverse.T.astype(jnp.bfloat16)
    return jnp.dot(filtered.astype(jnp.float32), factor.astype(jnp.float32), preferred_element_type=jnp.float32).astype(jnp.bfloat16)
```

```python
import functools

import jax
import jax.numpy as jnp
from jax import lax
from jax.experimental import pallas as pl
from jax.experimental.pallas import tpu as pltpu
from jax.sharding import PartitionSpec as P

CABLE_ROWS = 2304
MESH = pl.DeviceIdType.MESH
PAD = 8


NB = 128
HI = lax.Precision.HIGHEST


def spread(tile, lane):
    return jnp.broadcast_to(tile[:, lane : lane + 1], tile.shape)


def eliminate(block):
    lane = lax.broadcasted_iota(jnp.int32, (8, NB), 1)
    sub = lax.broadcasted_iota(jnp.int32, (8, NB), 0)
    tiles = NB // 8
    left = [block[8 * t : 8 * t + 8, :] for t in range(tiles)]
    right = [jnp.where(lane == sub + 8 * t, 1.0, 0.0).astype(jnp.float32) for t in range(tiles)]
    for g in range(tiles):
        home, away = left[g], right[g]
        column = [spread(home, 8 * g + i) for i in range(8)]
        scales, rows = [], []
        for i in range(8):
            scale = lax.rsqrt(column[i][i : i + 1, :])
            scales.append(scale)
            column[i] = column[i] * scale
            rows.append([column[i][n : n + 1, :] for n in range(8)])
            for n in range(i + 1, 8):
                column[n] = column[n] - column[i] * rows[i][n]
        for i in range(8):
            upper = home[i : i + 1, :] * scales[i]
            inverse = away[i : i + 1, :] * scales[i]
            home = jnp.where(sub > i, home - column[i] * upper, jnp.where(sub == i, upper, home))
            away = jnp.where(sub > i, away - column[i] * inverse, jnp.where(sub == i, inverse, away))
        right[g] = away
        for t in range(g + 1, tiles):
            factor = [spread(left[t], 8 * g + i) for i in range(8)]
            for i in range(8):
                factor[i] = factor[i] * scales[i]
                for n in range(i + 1, 8):
                    factor[n] = factor[n] - factor[i] * rows[i][n]
            for i in range(8):
                left[t] = left[t] - factor[i] * home[i : i + 1, :]
                right[t] = right[t] - factor[i] * away[i : i + 1, :]
    return jnp.concatenate(right, axis=0)


def mm(a, b, dims):
    return lax.dot_general(a, b, (dims, ((), ())), precision=HI, preferred_element_type=jnp.float32)


GROUPS = {
    "a": ((0, 0),),
    "b": ((1, 0), (1, 1)),
    "c": ((2, 0), (2, 1)),
    "d": ((2, 2), (3, 2), (3, 3)),
    "e": ((3, 0), (3, 1)),
}
OWNER = {"a": 3, "b": 2, "c": 2, "d": 2, "e": 2}
FOLDS = (("a", 0), ("b", 1), ("d", 2), ("c", 1), ("c", 2), ("e", 1), ("e", 2))
TRIPS = (
    (0, 1, 0, "all"),
    (0, 2, 0, "head"),
    (1, 2, 1, "head"),
    (2, 1, 2, "tail"),
    (2, 1, 3, "tail"),
    (3, 2, 3, "all"),
    (2, 3, 2, "all"),
    (2, 3, 0, "head"),
    (2, 3, 1, "head"),
    (1, 2, 0, "tail"),
    (1, 2, 1, "tail"),
    (2, 3, 0, "tail"),
    (2, 3, 1, "tail"),
)


def split_three(value):
    high = value.astype(jnp.bfloat16)
    rest = value - high.astype(jnp.float32)
    middle = rest.astype(jnp.bfloat16)
    low = (rest - middle.astype(jnp.float32)).astype(jnp.bfloat16)
    return jnp.concatenate([high, middle, low], axis=0)


def groups_of(parts, width):
    info = {}
    at = 0
    for name, blocks in GROUPS.items():
        unit = -(-(len(blocks) * width) // (parts * 8)) * 8
        info[name] = (at, unit, unit * parts, len(blocks) * width)
        at += unit * parts
    folds = {}
    deep = 0
    for number, (name, _) in enumerate(FOLDS):
        folds[number] = deep
        deep += info[name][1]
    return info, at, folds, deep


def kernel(
    parts,
    splits,
    x_any,
    mass_any,
    stiff_any,
    nodes_any,
    rigid_any,
    rows_any,
    spring_any,
    low_any,
    top_any,
    out_ref,
    x_ref,
    mass_ref,
    stiff_ref,
    nodes_ref,
    rigid_ref,
    rows_ref,
    spring_ref,
    low_ref,
    top_ref,
    value_ref,
    first_ref,
    link_ref,
    diag_ref,
    hot_ref,
    force_ref,
    send_buf,
    recv_buf,
    cols_ref,
    part_ref,
    fold_ref,
    all_ref,
    inv_ref,
    fac_ref,
    load_sem,
    ex_send,
    ex_recv,
    trip_send,
    trip_recv,
    fold_send,
    fold_recv,
    give_send,
    give_recv,
    row_send,
    row_recv,
):
    me = lax.axis_index("rows")
    col = lax.axis_index("vecs")
    count, width = x_ref.shape
    slots = rows_ref.shape[1]
    total_rows = count * parts
    unroll = parts <= 8

    barrier = pltpu.get_barrier_semaphore()
    for k in range(1, splits):
        pl.semaphore_signal(
            barrier, inc=1, device_id=(me, lax.rem(col + k, splits)), device_id_type=MESH
        )

    def greet(k, carry):
        pl.semaphore_signal(
            barrier, inc=1, device_id=(lax.rem(me + k, parts), col), device_id_type=MESH
        )
        return carry

    lax.fori_loop(1, parts, greet, 0)

    loads = [
        pltpu.make_async_copy(source, target, load_sem.at[n])
        for n, (source, target) in enumerate(
            [
                (x_any, x_ref),
                (mass_any, mass_ref),
                (stiff_any, stiff_ref),
                (nodes_any, nodes_ref),
                (rigid_any, rigid_ref),
                (rows_any, rows_ref),
                (spring_any, spring_ref),
                (low_any, low_ref),
                (top_any, top_ref),
            ]
        )
    ]
    for load in loads:
        load.start()

    chunk = count // splits
    zero_pad = jnp.zeros((PAD, width), jnp.float32)
    for ref in (value_ref, first_ref, link_ref):
        ref[0:PAD, :] = zero_pad
        ref[PAD + count :, :] = zero_pad
    force_ref[...] = jnp.zeros_like(force_ref)
    for load in loads:
        load.wait()

    top = jnp.full((1, width), top_ref[0], jnp.float32)
    bottom = jnp.full((1, width), low_ref[0], jnp.float32)
    center = (top + bottom) * 0.5
    inverse_half = 1.0 / ((top - bottom) * 0.5)

    for lo in range(0, count, chunk):
        value_ref[PAD + lo : PAD + lo + chunk, :] = x_ref[lo : lo + chunk, :].astype(jnp.float32)

    def remote(turn, k, target):
        return pltpu.make_async_remote_copy(
            src_ref=send_buf.at[turn, target],
            dst_ref=recv_buf.at[turn, me],
            send_sem=ex_send.at[turn, k],
            recv_sem=ex_recv.at[turn, k],
            device_id=(target, col),
            device_id_type=MESH,
        )

    def arrival(turn, k):
        source = lax.rem(me + parts - k, parts)
        return pltpu.make_async_remote_copy(
            src_ref=send_buf.at[turn, source],
            dst_ref=recv_buf.at[turn, source],
            send_sem=ex_send.at[turn, k],
            recv_sem=ex_recv.at[turn, k],
            device_id=(source, col),
            device_id_type=MESH,
        )

    def pick_anchors(turn, ref):
        first_row = ref[PAD + CABLE_ROWS : PAD + CABLE_ROWS + 1, :]
        last_row = ref[PAD + count - 1 : PAD + count, :]
        blank = jnp.zeros((8 - slots - 2, width), jnp.float32)

        def pick(q, carry):
            picked = [
                ref[pl.ds(PAD + jnp.minimum(rows_ref[0, s, q], count - 1), 1), :] for s in range(slots)
            ]
            send_buf[turn, q] = jnp.concatenate(picked + [first_row, last_row, blank], axis=0)
            return carry

        lax.fori_loop(0, parts, pick, 0, unroll=unroll)

    def push_anchors(turn):
        def push(k, carry):
            remote(turn, k, lax.rem(me + k, parts)).start()
            return carry

        lax.fori_loop(1, parts, push, 0, unroll=unroll)
        recv_buf[turn, me] = send_buf[turn, me]

    def collect(turn, scale):
        def take(k, carry):
            arrival(turn, k).wait_recv()
            return carry

        lax.fori_loop(1, parts, take, 0, unroll=unroll)

        def pull(q, carry):
            difference = send_buf[turn, q] - recv_buf[turn, q]
            for s in range(slots):
                live = jnp.where(rows_ref[0, s, q] < count, spring_ref[0, s, q], 0.0)
                force_ref[pl.ds(q * slots + s, 1), :] = live * difference[s : s + 1, :]
            return carry

        lax.fori_loop(0, parts, pull, 0, unroll=unroll)
        before = recv_buf[turn, lax.rem(me + parts - 1, parts)]
        after = recv_buf[turn, lax.rem(me + 1, parts)]
        own = send_buf[turn, me]
        left_open = jnp.where(me > 0, rigid_ref[0], 0.0)
        right_open = jnp.where(me < parts - 1, rigid_ref[0], 0.0)
        edge = jnp.concatenate(
            [
                left_open * (own[slots : slots + 1] - before[slots + 1 : slots + 2]),
                right_open * (own[slots + 1 : slots + 2] - after[slots : slots + 1]),
                jnp.zeros((6, width), jnp.float32),
            ],
            axis=0,
        )
        force_ref[parts * slots : parts * slots + 8, :] = edge
        return split_three(force_ref[...] * scale)

    pick_anchors(0, value_ref)

    forces = force_ref.shape[0]
    order = lax.rem(lax.broadcasted_iota(jnp.int32, (1, 3 * forces), 1), forces)
    ends = parts * slots
    target = jnp.where(order == ends, CABLE_ROWS, jnp.where(order == ends + 1, count - 1, count))

    def place_anchor(q, carry):
        for s in range(slots):
            carry = jnp.where(order == q * slots + s, rows_ref[0, s, q], carry)
        return carry

    target = lax.fori_loop(0, parts, place_anchor, target, unroll=unroll)

    lane = lax.broadcasted_iota(jnp.int32, (1, width), 1)
    rigid = rigid_ref[0]
    cuts = []
    running = nodes_ref[0, 0]
    for j in range(1, nodes_ref.shape[1]):
        cuts.append(running)
        running = running + nodes_ref[0, j]
    cuts.append(running)
    for r in range(count // width):
        place = lane + r * width
        open_link = place < CABLE_ROWS - 1
        for cut in cuts:
            open_link = open_link & (place + 1 != cut)
        deck_link = (place >= CABLE_ROWS) & (place < count - 1)
        link = jnp.where(open_link, stiff_ref[r : r + 1, :], jnp.where(deck_link, rigid, 0.0))
        lo = PAD + r * width
        link_ref[lo : lo + width, :] = jnp.broadcast_to(link, (width, width)).T
        mass = mass_ref[r : r + 1, :] - center
        diag_ref[r * width : (r + 1) * width, :] = jnp.broadcast_to(mass, (width, width)).T

    def base(ref, lo):
        at = PAD + lo
        here = ref[at : at + chunk, :]
        down = link_ref[at : at + chunk, :] * (here - ref[at + 1 : at + chunk + 1, :])
        up = link_ref[at - 1 : at + chunk - 1, :] * (here - ref[at - 1 : at + chunk - 1, :])
        return diag_ref[lo : lo + chunk, :] * here + down + up

    for lo in range(0, count, chunk):
        first_ref[PAD + lo : PAD + lo + chunk, :] = base(value_ref, lo) * inverse_half
        node = lax.broadcasted_iota(jnp.int32, (chunk, 3 * forces), 0) + lo
        hot_ref[lo : lo + chunk, :] = jnp.where(node == target, 1.0, 0.0).astype(jnp.bfloat16)

    pl.semaphore_wait(barrier, parts - 1 + splits - 1)
    push_anchors(0)
    pulls = collect(0, inverse_half)
    for lo in range(0, count, chunk):
        first_ref[PAD + lo : PAD + lo + chunk, :] += jnp.dot(
            hot_ref[lo : lo + chunk, :], pulls, preferred_element_type=jnp.float32
        )
    pick_anchors(1, first_ref)
    push_anchors(1)
    double = 2.0 * inverse_half
    for lo in range(0, count, chunk):
        diag_ref[lo : lo + chunk, :] = (
            base(first_ref, lo) * double - value_ref[PAD + lo : PAD + lo + chunk, :]
        )
    pulls = collect(1, double)

    def inner(left, right):
        return lax.dot_general(
            left, right, (((0,), (0,)), ((), ())), preferred_element_type=jnp.float32
        )

    own_gram = jnp.zeros((width, width), jnp.float32)
    for lo in range(0, count, chunk):
        made = (
            diag_ref[lo : lo + chunk, :]
            + jnp.dot(hot_ref[lo : lo + chunk, :], pulls, preferred_element_type=jnp.float32)
        ).astype(jnp.bfloat16)
        cols_ref[col, lo : lo + chunk, :] = made
        own_gram = own_gram + inner(made, made)

    info, _, folds, _ = groups_of(parts, width)
    upper = count // 3

    def trip(number):
        _, target, block, place = TRIPS[number]
        lo, size = {"all": (0, count), "head": (0, upper), "tail": (upper, count - upper)}[place]
        return pltpu.make_async_remote_copy(
            src_ref=cols_ref.at[block, pl.ds(lo, size)],
            dst_ref=cols_ref.at[block, pl.ds(lo, size)],
            send_sem=trip_send.at[number],
            recv_sem=trip_recv.at[number],
            device_id=(me, target),
            device_id_type=MESH,
        )

    def fold(number, source, target, k):
        name, _ = FOLDS[number]
        at, unit, _, _ = info[name]
        return pltpu.make_async_remote_copy(
            src_ref=part_ref.at[pl.ds(pl.multiple_of(at + target * unit, 8), unit)],
            dst_ref=fold_ref.at[source, pl.ds(folds[number], unit)],
            send_sem=fold_send.at[number, k],
            recv_sem=fold_recv.at[number, k],
            device_id=(target, OWNER[name]),
            device_id_type=MESH,
        )

    def skip(number):
        name, source = FOLDS[number]
        return 1 if source == OWNER[name] else 0

    def fold_start(number):
        def act(k, carry):
            fold(number, me, lax.rem(me + k, parts), k).start()
            return carry

        lax.fori_loop(skip(number), parts, act, 0, unroll=unroll)

    def fold_end(number):
        def act(k, carry):
            fold(number, me, lax.rem(me + k, parts), k).wait_send()
            return carry

        lax.fori_loop(skip(number), parts, act, 0, unroll=unroll)

    def place_of(name, owner):
        at, unit, _, _ = info[name]
        return pl.ds(pl.multiple_of(at + owner * unit, 8), unit)

    def fold_sum(name, numbers):
        _, unit, _, _ = info[name]
        total = jnp.zeros((unit, width), jnp.float32)
        for number in numbers:
            if skip(number):
                total = total + part_ref[place_of(name, me), :]

            def act(k, carry):
                source = lax.rem(me + parts - k, parts)
                fold(number, source, me, k).wait_recv()
                return carry + fold_ref[source, folds[number] : folds[number] + unit, :]

            total = lax.fori_loop(skip(number), parts, act, total, unroll=unroll)
        all_ref[place_of(name, me), :] = total

    def give(name, owner, target, k):
        n = list(GROUPS).index(name)
        return pltpu.make_async_remote_copy(
            src_ref=all_ref.at[place_of(name, owner)],
            dst_ref=all_ref.at[place_of(name, owner)],
            send_sem=give_send.at[n, k],
            recv_sem=give_recv.at[n, k],
            device_id=(target, splits - 1),
            device_id_type=MESH,
        )

    def give_skip(name):
        return 1 if OWNER[name] == splits - 1 else 0

    def give_start(name):
        def act(k, carry):
            give(name, me, lax.rem(me + k, parts), k).start()
            return carry

        lax.fori_loop(give_skip(name), parts, act, 0, unroll=unroll)

    def give_end(name):
        def act(k, carry):
            give(name, me, lax.rem(me + k, parts), k).wait_send()
            return carry

        lax.fori_loop(give_skip(name), parts, act, 0, unroll=unroll)

    def give_take(name):
        def act(k, carry):
            give(name, lax.rem(me + parts - k, parts), me, k).wait_recv()
            return carry

        lax.fori_loop(give_skip(name), parts, act, 0, unroll=unroll)

    def store_part(name, blocks):
        at, _, length, used = info[name]
        for n, block in enumerate(blocks):
            part_ref[at + n * width : at + (n + 1) * width, :] = block
        if used < length:
            part_ref[at + used : at + length, :] = jnp.zeros((length - used, width), jnp.float32)

    def factor_row(k):
        return pltpu.make_async_remote_copy(
            src_ref=fac_ref.at[k, :, pl.ds(0, (k + 1) * width)],
            dst_ref=fac_ref.at[k, :, pl.ds(0, (k + 1) * width)],
            send_sem=row_send.at[k],
            recv_sem=row_recv.at[k],
            device_id=(me, k),
            device_id_type=MESH,
        )

    def finish(device):
        used_width = (device + 1) * width
        factor = fac_ref[device, :, :used_width]
        for lo in range(0, count, chunk):
            block = jnp.concatenate(
                [cols_ref[b, lo : lo + chunk, :] for b in range(device + 1)], axis=1
            )
            out_ref[lo : lo + chunk, :] = lax.dot_general(
                block, factor, (((1,), (1,)), ((), ())), preferred_element_type=jnp.float32
            ).astype(jnp.bfloat16)

    def close(trips, numbers, names):
        for n in trips:
            trip(n).wait_send()
        for number in numbers:
            fold_end(number)
        for name in names:
            give_end(name)

    @pl.when(col == 0)
    def _():
        trip(0).start()
        store_part("a", [own_gram])
        fold_start(0)
        trip(1).start()
        factor_row(0).wait_recv()
        finish(0)
        close([0, 1], [0], [])

    @pl.when(col == 1)
    def _():
        trip(0).wait_recv()
        cross = jnp.zeros((width, width), jnp.float32)
        for lo in range(0, count, chunk):
            cross = cross + inner(cols_ref[1, lo : lo + chunk, :], cols_ref[0, lo : lo + chunk, :])
        store_part("b", [cross, own_gram])
        fold_start(1)
        trip(2).start()
        for number, block, name, fold_number, later in ((3, 2, "c", 3, 9), (4, 3, "e", 5, 10)):
            trip(number).wait_recv()
            cross = jnp.zeros((width, 2 * width), jnp.float32)
            for lo in range(upper, count, upper):
                cross = cross + inner(
                    cols_ref[block, lo : lo + upper, :],
                    jnp.concatenate(
                        [cols_ref[0, lo : lo + upper, :], cols_ref[1, lo : lo + upper, :]], axis=1
                    ),
                )
            store_part(name, [cross[:, :width], cross[:, width:]])
            fold_start(fold_number)
            trip(later).start()
        factor_row(1).wait_recv()
        finish(1)
        close([2, 9, 10], [1, 3, 5], [])

    @pl.when(col == 2)
    def _():
        trip(3).start()
        trip(6).start()
        trip(5).wait_recv()
        trip(4).start()
        cross = jnp.zeros((width, 2 * width), jnp.float32)
        for lo in range(0, count, chunk):
            third = cols_ref[3, lo : lo + chunk, :]
            cross = cross + inner(
                third, jnp.concatenate([cols_ref[2, lo : lo + chunk, :], third], axis=1)
            )
        store_part("d", [own_gram, cross[:, :width], cross[:, width:]])
        fold_start(2)
        fold_sum("b", [1])
        give_start("b")
        fold_sum("d", [2])
        give_start("d")
        trip(1).wait_recv()
        trip(2).wait_recv()
        pair = jnp.concatenate([cols_ref[0, :upper, :], cols_ref[1, :upper, :]], axis=1)
        cross = inner(jnp.concatenate([cols_ref[2, :upper, :], cols_ref[3, :upper, :]], axis=1), pair)
        store_part("c", [cross[:width, :width], cross[:width, width:]])
        fold_start(4)
        store_part("e", [cross[width:, :width], cross[width:, width:]])
        fold_start(6)
        trip(7).start()
        trip(8).start()
        fold_sum("c", [4, 3])
        give_start("c")
        fold_sum("e", [6, 5])
        give_start("e")
        trip(9).wait_recv()
        trip(11).start()
        trip(10).wait_recv()
        trip(12).start()
        factor_row(2).wait_recv()
        finish(2)
        close([3, 4, 6, 7, 8, 11, 12], [2, 4, 6], ["b", "c", "d", "e"])

    @pl.when(col == 3)
    def _():
        trip(5).start()
        inv_ref[...] = jnp.zeros_like(inv_ref)
        fold_sum("a", [0])
        give_start("a")
        blocks = {}
        for name, members in GROUPS.items():
            at = info[name][0]
            for n, member in enumerate(members):
                blocks[member] = at + n * width
        scale = 1.0 / total_rows

        def gram(i, j):
            at = blocks[i, j]
            return all_ref[at : at + width, :] * scale

        for k, names in enumerate(("a", "b", "dc", "e")):
            for name in names:
                give_take(name)
            lo, hi = k * width, (k + 1) * width
            rest = gram(k, k)
            if k:
                known = inv_ref[:lo, :lo]
                panel = mm(jnp.concatenate([gram(k, j) for j in range(k)], axis=1), known, ((1,), (1,)))
                rest = rest - mm(panel, panel, ((1,), (1,)))
                carried = mm(panel, known, ((1,), (0,)))
            corner = eliminate(rest)
            if k:
                side = -mm(corner, carried, ((1,), (0,)))
                inv_ref[lo:hi, :lo] = side
                fac_ref[k, :, :lo] = side.astype(jnp.bfloat16)
            inv_ref[lo:hi, lo:hi] = corner
            fac_ref[k, :, lo:hi] = corner.astype(jnp.bfloat16)
            if k < splits - 1:
                factor_row(k).start()
        for n in (6, 7, 8, 11, 12):
            trip(n).wait_recv()
        finish(splits - 1)
        close([5], [], ["a"])
        for k in range(splits - 1):
            factor_row(k).wait_send()

    def settle(k, carry):
        target = lax.rem(me + k, parts)
        remote(0, k, target).wait_send()
        remote(1, k, target).wait_send()
        return carry

    lax.fori_loop(1, parts, settle, 0, unroll=unroll)


def body(
    parts,
    splits,
    vectors,
    node_mass,
    cable_stiff,
    cable_nodes,
    deck_rigidity,
    anchor_rows,
    anchor_stiff,
    cut_low,
    top_bound,
):
    count, width = vectors.shape
    slots = anchor_rows.shape[2]
    forces = parts * slots + 8
    size = splits * width
    _, length, _, deep = groups_of(parts, width)
    sem = pltpu.SemaphoreType.DMA
    f32 = jnp.float32
    args = (
        vectors,
        node_mass.reshape(-1, width),
        cable_stiff.reshape(-1, width),
        cable_nodes,
        deck_rigidity.reshape(1),
        jnp.transpose(anchor_rows, (0, 2, 1)),
        jnp.transpose(anchor_stiff, (0, 2, 1)),
        cut_low.reshape(1),
        top_bound.reshape(1),
    )
    return pl.pallas_call(
        functools.partial(kernel, parts, splits),
        out_shape=jax.ShapeDtypeStruct((count, width), jnp.bfloat16),
        in_specs=[pl.BlockSpec(memory_space=pl.ANY)] * len(args),
        out_specs=pl.BlockSpec(memory_space=pltpu.VMEM),
        scratch_shapes=[pltpu.VMEM(a.shape, a.dtype) for a in args[:3]]
        + [pltpu.SMEM(a.shape, a.dtype) for a in args[3:]]
        + [
            pltpu.VMEM((count + 2 * PAD, width), f32),
            pltpu.VMEM((count + 2 * PAD, width), f32),
            pltpu.VMEM((count + 2 * PAD, width), f32),
            pltpu.VMEM((count, width), f32),
            pltpu.VMEM((count, 3 * forces), jnp.bfloat16),
            pltpu.VMEM((forces, width), f32),
            pltpu.VMEM((2, parts, 8, width), f32),
            pltpu.VMEM((2, parts, 8, width), f32),
            pltpu.VMEM((splits, count, width), jnp.bfloat16),
            pltpu.VMEM((length, width), f32),
            pltpu.VMEM((parts, deep, width), f32),
            pltpu.VMEM((length, width), f32),
            pltpu.VMEM((size, size), f32),
            pltpu.VMEM((splits, width, size), jnp.bfloat16),
            sem((len(args),)),
            sem((2, parts)),
            sem((2, parts)),
            sem((len(TRIPS),)),
            sem((len(TRIPS),)),
            sem((len(FOLDS), parts)),
            sem((len(FOLDS), parts)),
            sem((len(GROUPS), parts)),
            sem((len(GROUPS), parts)),
            sem((splits - 1,)),
            sem((splits - 1,)),
        ],
        compiler_params=pltpu.CompilerParams(
            collective_id=0, has_side_effects=True, vmem_limit_bytes=60 * 1024 * 1024
        ),
    )(*args)


def solution(mesh):
    return jax.shard_map(
        functools.partial(body, mesh.shape["rows"], mesh.shape["vecs"]),
        mesh=mesh,
        in_specs=(
            P("rows", "vecs"),
            P("rows"),
            P("rows"),
            P("rows", None),
            P(),
            P("rows", None, None),
            P("rows", None, None),
            P(),
            P(),
        ),
        out_specs=P("rows", "vecs"),
        check_vma=False,
    )
```
